32 devices in a mesh: inst: 2 (over core), lon: 16 (over z, y, x).
Axes of the slice: x: 2, y: 2, z: 4, core: 2. Of those that a mesh axis runs over, the one named last changes fastest.
Arguments:
- obs_x: bfloat16 [384, 128, 256], P(('inst', 'lon')), may hold values from -6 to 6
- obs_cot: bfloat16 [384, 128, 256], P(('inst', 'lon')), may hold values from -6 to 6
- tile_window: int32 [384, 2], P(('inst', 'lon')), may hold values from 0 to 179, as said below
- point_mask: int32 [384, 128], P(('inst', 'lon')), may hold values from 0 to 1, as said below
- band_counts: int32 [32], P(('inst', 'lon')), may hold values from 1 to 12, as said below
- latents: bfloat16 [64, 184, 256], P('lon'), may hold values from -6 to 6
- w_query: bfloat16 [256, 128], replicated, may hold values from -3 to 3
- w_key: bfloat16 [256, 128], replicated, may hold values from -0.375 to 0.375
- w_value: bfloat16 [256, 128], replicated, may hold values from -0.375 to 0.375
- w_out: bfloat16 [128, 256], replicated, may hold values from -0.5 to 0.5
Outputs:
- decoded: bfloat16 [384, 128, 256], P(('inst', 'lon'))
- obs_grad: bfloat16 [384, 128, 256], P(('inst', 'lon'))
- latent_grad: float32 [64, 184, 256], P('lon')
- query_grad: float32 [256, 128], replicated
- key_grad: float32 [256, 128], replicated
- value_grad: float32 [256, 128], replicated
- out_grad: float32 [128, 256], replicated
The draws below stay inside these ranges and needn't reach their ends.
Inputs may be any that keep to these rules, and one draw needn't show every extreme that they name: `tile_window`: column 0 is the first longitude column of the tile's window; the window's centre column (column 2) mod 64 is one of the 4 columns of the band that holds the tile. Column 1 is the window's first latitude row, at most 179. `point_mask`: in each tile the live slots come first, and half or more of the slots are live. `band_counts`: one entry equals 12.
All inputs are finite; a program needn't handle non-finite values.
Results may differ from the reference program's by a relative error of at most 0.007.
The reference program's roundings to bfloat16 on the way count: a program that leaves them out, or rounds other values in their place, can miss the bound.
Values may be sent and summed in bfloat16 or wider, within the bound.
A program may use at most 64 MiB of HBM per device.

```python
import math
import jax
import jax.numpy as jnp
from jax import lax

D = 256
HEADS = 4
ATTN = 128
TILE = 128
TILES_DEV = 12
LC_DEV = 4
NLAT = 184
REACH = 2
LONS = 64
TILES = 384
N_INST = 2
N_LON = 16


def draw_band_counts(key, part):
    devices_all = N_INST * N_LON
    first, second = jax.random.split(key)
    spread = jax.random.randint(first, (devices_all,), 0, TILES_DEV)
    counts = 1 + spread * spread // TILES_DEV
    fullest = jax.random.randint(second, (), 0, devices_all)
    return jnp.where(jnp.arange(devices_all) == fullest, TILES_DEV, counts).astype(jnp.int32)


def draw_point_mask(key, part):
    tile_total = TILES_DEV * N_INST * N_LON
    live_len = jax.random.randint(key, (tile_total, 1), TILE // 2, TILE + 1)
    return (jnp.arange(TILE)[None, :] < live_len).astype(jnp.int32)


def draw_tile_window(key, part):
    tile_total = TILES_DEV * N_INST * N_LON
    first, second = jax.random.split(jax.random.fold_in(key, 7))
    tile_ids = jnp.arange(tile_total)
    bands = tile_ids // TILES_DEV % N_LON
    offset = jax.random.randint(first, (tile_total,), 0, LC_DEV)
    offset = jnp.where(tile_ids == 0, REACH - 1, jnp.where(tile_ids == 1, REACH, offset))
    centre = bands * LC_DEV + offset
    column = (centre - REACH) % LONS
    lat_first = jax.random.randint(second, (tile_total,), 0, NLAT - 2 * REACH)
    lat_first = jnp.where(tile_ids == 0, NLAT - 2 * REACH - 1, jnp.where(tile_ids == 1, 0, lat_first))
    return jnp.stack([column, lat_first], axis=1).astype(jnp.int32)


def level_of(own_key, extent, cuts, least, top_value):
    level, own = 1.0, jax.random.fold_in(own_key, 6)
    for position, parts in cuts:
        draws = jnp.exp(jax.random.uniform(jax.random.fold_in(own, position), (parts,), jnp.float32, least / len(cuts), top_value / len(cuts)))
        level = level * jnp.repeat(draws, extent[position] // parts).reshape([-1 if axis == position else 1 for axis in range(len(extent))])
    return level


def centred(stream_key, shape, width, reach, cuts=(), kind=jnp.bfloat16):
    values = jax.random.normal(stream_key, shape, jnp.float32) * width
    if len(cuts) > 0:
        values = level_of(stream_key, shape, cuts, -0.22, 0.18) * values
    return jnp.clip(values, min=-reach, max=reach).astype(kind)


def setup_inputs(seed: int = 0) -> dict:
    streams_of = jax.random.split(jax.random.key(seed), 11)
    obs_x = centred(streams_of[0], (TILES, TILE, D), 1.0, 6.0, ((0, 32),))
    obs_cot = centred(streams_of[1], (TILES, TILE, D), 1.0, 6.0, ((0, 32),))
    tile_window = draw_tile_window(jax.random.fold_in(streams_of[10], 71), 0)
    point_mask = draw_point_mask(jax.random.fold_in(streams_of[10], 71), 0)
    band_counts = draw_band_counts(jax.random.fold_in(streams_of[10], 71), 0)
    latents = centred(streams_of[5], (LONS, NLAT, D), 1.0, 6.0, ((0, 16),))
    w_query = centred(streams_of[6], (D, ATTN), (D // 64) ** -0.5, 3.0)
    w_key = centred(streams_of[7], (D, ATTN), D ** -0.5, 0.375)
    w_value = centred(streams_of[8], (D, ATTN), D ** -0.5, 0.375)
    w_out = centred(streams_of[9], (ATTN, D), ATTN ** -0.5, 0.5)
    return {"obs_x": obs_x, "obs_cot": obs_cot, "tile_window": tile_window, "point_mask": point_mask, "band_counts": band_counts, "latents": latents, "w_query": w_query, "w_key": w_key, "w_value": w_value, "w_out": w_out}


softcap = 30.0

def split_products(grad, w_pair, flat_latents):
    grad_high = grad.astype(jnp.bfloat16)
    grad_low = (grad - grad_high.astype(jnp.float32)).astype(jnp.bfloat16)
    by_rows = (((1,), (1,)), ((), ()))
    by_cols = (((0,), (0,)), ((), ()))
    latent_part = lax.dot_general(grad_high, w_pair, by_rows, preferred_element_type=jnp.float32) + lax.dot_general(grad_low, w_pair, by_rows, preferred_element_type=jnp.float32)
    pair_weight = lax.dot_general(flat_latents, grad_high, by_cols, preferred_element_type=jnp.float32) + lax.dot_general(flat_latents, grad_low, by_cols, preferred_element_type=jnp.float32)
    return (latent_part, pair_weight)

def attend(obs_x, obs_cot, live_points, windows, w_query, w_out):
    n_tiles, tile_len, model_width = obs_x.shape
    attn_width = w_query.shape[1]
    head_size = attn_width // HEADS
    score_scale = 1.0 / math.sqrt(head_size)
    flat_x = obs_x.reshape(-1, model_width)
    queries = jnp.dot(flat_x, w_query, preferred_element_type=jnp.float32).astype(jnp.bfloat16)
    query_heads = queries.reshape(n_tiles, tile_len, HEADS, head_size)
    win_keys = windows[:, :, :attn_width].reshape(n_tiles, -1, HEADS, head_size)
    win_values = windows[:, :, attn_width:].reshape(n_tiles, -1, HEADS, head_size)
    raw_scores = jnp.einsum('nqhd,nkhd->nhqk', query_heads.astype(jnp.float32), win_keys.astype(jnp.float32)) * score_scale
    capped = softcap * jnp.tanh(raw_scores / softcap)
    weights = jnp.exp(capped)
    probs = weights / lax.optimization_barrier(jnp.sum(weights, axis=-1, keepdims=True))
    probs_b = probs.astype(jnp.bfloat16)
    attended = jnp.einsum('nhqk,nkhd->nqhd', probs_b.astype(jnp.float32), win_values.astype(jnp.float32))
    attended = attended.astype(jnp.bfloat16).reshape(-1, attn_width)
    projected = jnp.dot(attended, w_out, preferred_element_type=jnp.float32).reshape(n_tiles, tile_len, model_width)
    decoded = (obs_x.astype(jnp.float32) + live_points[:, :, None] * projected).astype(jnp.bfloat16)
    masked = obs_cot * live_points.astype(jnp.bfloat16)[:, :, None]
    flat_cot = masked.reshape(-1, model_width)
    out_grad = jnp.dot(attended.T, flat_cot, preferred_element_type=jnp.float32)
    attended_grad = jnp.dot(flat_cot, w_out.T, preferred_element_type=jnp.float32).astype(jnp.bfloat16)
    attended_grad = attended_grad.reshape(n_tiles, tile_len, HEADS, head_size)
    prob_grad = jnp.einsum('nqhd,nkhd->nhqk', attended_grad.astype(jnp.float32), win_values.astype(jnp.float32))
    row_inner = lax.optimization_barrier(jnp.sum(probs * prob_grad, axis=-1, keepdims=True))
    score_grad = (probs * (prob_grad - row_inner) * (1.0 - (capped / softcap) ** 2) * score_scale).astype(jnp.bfloat16)
    query_part = jnp.einsum('nhqk,nkhd->nqhd', score_grad.astype(jnp.float32), win_keys.astype(jnp.float32))
    query_part = query_part.astype(jnp.bfloat16).reshape(-1, attn_width)
    key_part = jnp.einsum('nhqk,nqhd->nkhd', score_grad.astype(jnp.float32), query_heads.astype(jnp.float32))
    value_part = jnp.einsum('nhqk,nqhd->nkhd', probs_b.astype(jnp.float32), attended_grad.astype(jnp.float32))
    window_grad = jnp.concatenate([key_part.reshape(n_tiles, -1, attn_width), value_part.reshape(n_tiles, -1, attn_width)], axis=-1)
    obs_grad = obs_cot.astype(jnp.float32).reshape(-1, model_width) + jnp.dot(query_part, w_query.T, preferred_element_type=jnp.float32)
    obs_grad = obs_grad.astype(jnp.bfloat16).reshape(n_tiles, tile_len, model_width)
    query_grad = jnp.dot(flat_x.T, query_part, preferred_element_type=jnp.float32)
    return (decoded, obs_grad, window_grad, query_grad, out_grad)

def reference(obs_x, obs_cot, tile_window, point_mask, band_counts, latents, w_query, w_key, w_value, w_out):
    lon_cols, lat_rows, model_width = latents.shape
    attn_width = w_query.shape[1]
    window = 2 * REACH + 1
    w_pair = jnp.concatenate([w_key, w_value], axis=1)
    flat_latents = latents.reshape(-1, model_width)
    pairs = jnp.dot(flat_latents, w_pair, preferred_element_type=jnp.float32).astype(jnp.bfloat16)
    offsets = jnp.arange(window, dtype=jnp.int32)
    columns = (tile_window[:, 0:1] + offsets[None, :]) % lon_cols
    lat_index = tile_window[:, 1:2] + offsets[None, :]
    key_index = (columns[:, :, None] * lat_rows + lat_index[:, None, :]).reshape(-1, window * window).astype(jnp.int32)
    tile_total, tile_len = point_mask.shape
    device_total = tile_total // TILES_DEV
    local_tile = jnp.arange(tile_total, dtype=jnp.int32) % TILES_DEV
    counts = jnp.repeat(band_counts, TILES_DEV, total_repeat_length=tile_total)
    live_points = point_mask.astype(jnp.float32) * (local_tile < counts).astype(jnp.float32)[:, None]

    def per_device(device_block):
        block_x, block_cot, block_live, block_index = device_block
        windows = jnp.take(pairs, block_index, axis=0)
        return attend(block_x, block_cot, block_live, windows, w_query, w_out)
    results = lax.map(per_device, (obs_x.reshape(device_total, TILES_DEV, tile_len, model_width), obs_cot.reshape(device_total, TILES_DEV, tile_len, model_width), live_points.reshape(device_total, TILES_DEV, tile_len), key_index.reshape(device_total, TILES_DEV, window * window)))
    decoded = results[0].reshape(obs_x.shape)
    obs_grad = results[1].reshape(obs_x.shape)
    window_grad = results[2].reshape(-1, 2 * attn_width)
    query_grad = lax.optimization_barrier(jnp.sum(results[3], axis=0))
    out_grad = lax.optimization_barrier(jnp.sum(results[4], axis=0))
    pair_grad = jnp.zeros((lon_cols * lat_rows, 2 * attn_width), jnp.float32).at[key_index.reshape(-1)].add(window_grad)
    latent_grad, pair_weight = split_products(pair_grad, w_pair, flat_latents)
    return (decoded, obs_grad, latent_grad.reshape(lon_cols, lat_rows, model_width), query_grad, pair_weight[:, :attn_width], pair_weight[:, attn_width:], out_grad)
```

```python
import functools
import math

import jax
import jax.numpy as jnp
from jax import lax
from jax.experimental import pallas as pl
from jax.experimental.pallas import tpu as pltpu
from jax.sharding import PartitionSpec as P

HEADS = 4
REACH = 2
WINDOW = 2 * REACH + 1
SUB = 8
CAP = 30.0
MESH = pl.DeviceIdType.MESH
F32 = jnp.float32
BF16 = jnp.bfloat16

NT = (((1,), (1,)), ((), ()))
TN = (((0,), (0,)), ((), ()))


def dot(a, b, dims=(((1,), (0,)), ((), ()))):
    return lax.dot_general(a, b, dims, preferred_element_type=F32)


def halo_kernel(n_lon, lat, low, high, send, recv):
    me = lax.axis_index("lon")
    right, left = lax.rem(me + 1, n_lon), lax.rem(me + n_lon - 1, n_lon)
    barrier = pltpu.get_barrier_semaphore()
    for other in (left, right):
        pl.semaphore_signal(barrier, inc=1, device_id={"lon": other}, device_id_type=MESH)
    pl.semaphore_wait(barrier, 2)
    edge = low.shape[0]
    rows = lat.shape[0]
    up = pltpu.make_async_remote_copy(
        src_ref=lat.at[pl.ds(rows - edge, edge)], dst_ref=low, send_sem=send.at[0],
        recv_sem=recv.at[0], device_id={"lon": right}, device_id_type=MESH)
    down = pltpu.make_async_remote_copy(
        src_ref=lat.at[pl.ds(0, edge)], dst_ref=high, send_sem=send.at[1],
        recv_sem=recv.at[1], device_id={"lon": left}, device_id_type=MESH)
    up.start()
    down.start()
    up.wait()
    down.wait()


def attend_kernel(
    lon_cols, lat_rows, tw, cnt, x_ref, cot_ref, mask_ref, lat, low, high, wq, wk, wv, wo,
    dec, og, own_out, halo_out, g_out, keys, values, kg, vg, qg, outg,
):
    step = pl.program_id(0)
    tiles, length, width = x_ref.shape
    attn = wq.shape[1]
    head = attn // HEADS
    scale = 1.0 / math.sqrt(head)
    own_rows, edge = lat.shape[0], low.shape[0]
    wide = own_rows + 2 * edge
    slots = WINDOW * SUB
    band_cols = own_rows // lat_rows

    @pl.when(step == 0)
    def _():
        w_pair = jnp.concatenate([wk[...], wv[...]], axis=1)

        def project(block):
            return dot(block[...], w_pair).astype(BF16).astype(F32)

        for ref, first, count in ((low, 0, edge), (lat, edge, own_rows), (high, edge + own_rows, edge)):
            block = project(ref)
            keys[pl.ds(first, count), :] = block[:, :attn]
            values[pl.ds(first, count), :] = block[:, attn:]
        keys[pl.ds(wide, SUB), :] = jnp.zeros((SUB, attn), F32)
        values[pl.ds(wide, SUB), :] = jnp.zeros((SUB, attn), F32)
        kg[...] = jnp.zeros_like(kg)
        vg[...] = jnp.zeros_like(vg)
        qg[...] = jnp.zeros_like(qg)
        outg[...] = jnp.zeros_like(outg)

    flat_x = x_ref[...].reshape(tiles * length, width)
    flat_cot = cot_ref[...].reshape(tiles * length, width)
    queries = dot(flat_x, wq[...]).astype(BF16)

    row_id = lax.broadcasted_iota(jnp.int32, (length, width), 0)
    lives = []
    for j in range(tiles):
        t = step * tiles + j
        used = jnp.sum(mask_ref[pl.ds(t, 1), :], axis=1, keepdims=True)
        used = jnp.where(t < cnt[0], used, 0)
        lives.append(row_id < used)
    live = jnp.concatenate([m.astype(F32) for m in lives], axis=0)
    masked = (flat_cot.astype(F32) * live).astype(BF16)
    att_grad = dot(masked, wo[...], NT).astype(BF16)

    lane = lax.broadcasted_iota(jnp.int32, (1, attn), 1) // head
    head_mask = [(lane == h).astype(F32) for h in range(HEADS)]
    slot_id = lax.broadcasted_iota(jnp.int32, (slots, length), 0)
    valid = ((slot_id & (SUB - 1)) < WINDOW)[None]
    band_first = lax.axis_index("lon") * band_cols

    att_parts, query_parts = [], []
    for j in range(tiles):
        t = step * tiles + j
        col = lax.rem(tw[t, 0] - band_first + REACH + lon_cols, lon_cols)
        base = col * lat_rows + tw[t, 1]
        q_t = queries[j * length : (j + 1) * length]
        g_t = att_grad[j * length : (j + 1) * length]
        spans = [pl.ds(base + a * lat_rows, SUB) for a in range(WINDOW)]
        kw = jnp.concatenate([keys[at, :] for at in spans], axis=0)
        vw = jnp.concatenate([values[at, :] for at in spans], axis=0)
        kb = jnp.concatenate([kw * m for m in head_mask], axis=0).astype(BF16)
        vb = jnp.concatenate([vw * m for m in head_mask], axis=0).astype(BF16)
        th = jnp.tanh(dot(kb, q_t, NT) * scale / CAP).reshape(HEADS, slots, length)
        e = jnp.where(valid, jnp.exp(CAP * th), 0.0)
        p = e * (1.0 / jnp.sum(e, axis=1, keepdims=True))
        dp = dot(vb, g_t, NT).reshape(HEADS, slots, length)
        inner = jnp.sum(p * dp, axis=1, keepdims=True)
        sg = p * (dp - inner) * (1.0 - th * th) * scale
        sg = sg.reshape(HEADS * slots, length).astype(BF16)
        pb = p.reshape(HEADS * slots, length).astype(BF16)
        att_parts.append(dot(pb, vb, TN).astype(BF16))
        query_parts.append(dot(sg, kb, TN).astype(BF16))
        kp = dot(sg, q_t)
        vp = dot(pb, g_t)
        k_sum = sum(kp[h * slots : (h + 1) * slots] * head_mask[h] for h in range(HEADS))
        v_sum = sum(vp[h * slots : (h + 1) * slots] * head_mask[h] for h in range(HEADS))
        for a, at in enumerate(spans):
            kg[at, :] = kg[at, :] + k_sum[a * SUB : (a + 1) * SUB]
            vg[at, :] = vg[at, :] + v_sum[a * SUB : (a + 1) * SUB]

    attended = jnp.concatenate(att_parts, axis=0)
    query_part = jnp.concatenate(query_parts, axis=0)
    dec[...] = (flat_x.astype(F32) + live * dot(attended, wo[...])).astype(BF16).reshape(dec.shape)
    og[...] = (flat_cot.astype(F32) + dot(query_part, wq[...], NT)).astype(BF16).reshape(og.shape)
    qg[...] += dot(flat_x, query_part, TN)
    outg[...] += dot(attended, masked, TN)

    @pl.when(step == pl.num_programs(0) - 1)
    def _():
        for ref, lanes in ((kg, pl.ds(0, attn)), (vg, pl.ds(attn, attn))):
            own_out[:, lanes] = ref[pl.ds(edge, own_rows), :]
            halo_out[pl.ds(0, edge), lanes] = ref[pl.ds(0, edge), :].astype(BF16)
            halo_out[pl.ds(edge, edge), lanes] = ref[pl.ds(edge + own_rows, edge), :].astype(BF16)
        kv = jnp.zeros((width, 2 * attn), F32)
        for ref, first, count in ((low, 0, edge), (lat, edge, own_rows), (high, edge + own_rows, edge)):
            rows_at = pl.ds(first, count)
            grad = jnp.concatenate([kg[rows_at, :], vg[rows_at, :]], axis=1)
            grad_high = grad.astype(BF16)
            grad_low = (grad - grad_high.astype(F32)).astype(BF16)
            kv = kv + dot(ref[...], grad_high, TN) + dot(ref[...], grad_low, TN)
        rows = g_out.shape[1]
        pieces = (qg[...], kv[:, :attn], kv[:, attn:], outg[:, :attn], outg[:, attn:])
        at = 0
        for piece in pieces:
            count = piece.shape[0] // rows
            g_out[pl.ds(at, count)] = piece.astype(BF16).reshape(count, rows, attn)
            at += count


def reduce_kernel(
    n_inst, n_lon, own, halo, g, wk, wv, lat_out, q_out, k_out, v_out, o_out,
    hbuf, shares, rs, part, ag, h_s, h_r, i_s, i_r, rs_s, rs_r, p_s, p_r, a_s, a_r,
):
    me, mi = lax.axis_index("lon"), lax.axis_index("inst")
    edge = hbuf.shape[1]
    own_rows = own.shape[0]
    attn = wk.shape[1]

    def lon_at(d):
        return lax.rem(me + d, n_lon)

    def inst_at(d):
        return lax.rem(mi + d, n_inst)

    barrier = pltpu.get_barrier_semaphore()
    for d in range(1, n_lon):
        pl.semaphore_signal(barrier, inc=1, device_id={"lon": lon_at(d)}, device_id_type=MESH)
    for d in range(1, n_inst):
        pl.semaphore_signal(barrier, inc=1, device_id={"inst": inst_at(d)}, device_id_type=MESH)
    pl.semaphore_wait(barrier, n_lon + n_inst - 2)

    def send(src, dst, s, r, target):
        copy = pltpu.make_async_remote_copy(
            src_ref=src, dst_ref=dst, send_sem=s, recv_sem=r, device_id=target,
            device_id_type=MESH)
        copy.start()
        return copy

    halos = [
        send(halo.at[pl.ds(0, edge)], hbuf.at[0], h_s.at[0], h_r.at[0], {"lon": lon_at(n_lon - 1)}),
        send(halo.at[pl.ds(edge, edge)], hbuf.at[1], h_s.at[1], h_r.at[1], {"lon": lon_at(1)}),
    ]
    scatters = [
        send(g.at[lon_at(d)], rs.at[d], rs_s.at[d], rs_r.at[d], {"lon": lon_at(d)})
        for d in range(1, n_lon)
    ]
    for copy in scatters:
        copy.wait()
    total = g[me].astype(F32)
    for d in range(1, n_lon):
        total = total + rs[d].astype(F32)
    part[mi] = total
    swaps = [
        send(part.at[mi], part.at[mi], p_s.at[d], p_r.at[d], {"inst": inst_at(d)})
        for d in range(1, n_inst)
    ]
    for copy in halos:
        copy.wait()
    shares[mi, pl.ds(0, edge), :] = (own[pl.ds(0, edge), :] + hbuf[1].astype(F32)).astype(BF16)
    shares[mi, pl.ds(own_rows - edge, edge), :] = (
        own[pl.ds(own_rows - edge, edge), :] + hbuf[0].astype(F32)
    ).astype(BF16)
    joins = [
        send(shares.at[mi], shares.at[mi], i_s.at[d], i_r.at[d], {"inst": inst_at(d)})
        for d in range(1, n_inst)
    ]
    for copy in swaps:
        copy.wait()
    total = part[0]
    for i in range(1, n_inst):
        total = total + part[i]
    ag[me] = total.astype(BF16)
    gathers = [
        send(ag.at[me], ag.at[me], a_s.at[d], a_r.at[d], {"lon": lon_at(d)})
        for d in range(1, n_lon)
    ]
    for copy in joins:
        copy.wait()
    grad = shares[0].astype(F32)
    for i in range(1, n_inst):
        grad = grad + shares[i].astype(F32)
    grad_high = grad.astype(BF16)
    grad_low = (grad - grad_high.astype(F32)).astype(BF16)
    w_pair = jnp.concatenate([wk[...], wv[...]], axis=1)
    lat_out[...] = dot(grad_high, w_pair, NT) + dot(grad_low, w_pair, NT)
    for copy in gathers:
        copy.wait()
    rows = ag.shape[1]
    at = 0

    def take(count):
        nonlocal at
        block = ag[pl.ds(at, count // rows)].astype(F32).reshape(count, attn)
        at += count // rows
        return block

    q_out[...] = take(q_out.shape[0])
    k_out[...] = take(k_out.shape[0])
    v_out[...] = take(v_out.shape[0])
    o_out[:, pl.ds(0, attn)] = take(o_out.shape[0])
    o_out[:, pl.ds(attn, attn)] = take(o_out.shape[0])


def vmem():
    return pl.BlockSpec(memory_space=pltpu.VMEM)


def shards(
    n_inst, n_lon, obs_x, obs_cot, tile_window, point_mask, band_counts, latents,
    w_query, w_key, w_value, w_out,
):
    n_tiles, length, width = obs_x.shape
    band_cols, lat_rows, _ = latents.shape
    attn = w_query.shape[1]
    edge, own_rows = REACH * lat_rows, band_cols * lat_rows
    wide = own_rows + 2 * edge
    flat = latents.reshape(own_rows, width)
    dma = pltpu.SemaphoreType.DMA
    low, high = pl.pallas_call(
        functools.partial(halo_kernel, n_lon),
        out_shape=[jax.ShapeDtypeStruct((edge, width), BF16)] * 2,
        in_specs=[pl.BlockSpec(memory_space=pl.ANY)],
        out_specs=[pl.BlockSpec(memory_space=pl.ANY)] * 2,
        scratch_shapes=[dma((2,)), dma((2,))],
        compiler_params=pltpu.CompilerParams(collective_id=0, has_side_effects=True),
        name="halo",
    )(flat)

    group = next(b for b in (4, 3, 2, 1) if n_tiles % b == 0)
    weight_rows = 2 * width + 2 * attn + width
    rows = weight_rows // n_lon
    whole = lambda *shape: pl.BlockSpec(shape, lambda i: (0,) * len(shape))
    tile_spec = pl.BlockSpec((group, length, width), lambda i: (i, 0, 0))
    smem = pl.BlockSpec(memory_space=pltpu.SMEM)
    decoded, obs_grad, own, halo, g = pl.pallas_call(
        functools.partial(attend_kernel, band_cols * n_lon, lat_rows),
        grid=(n_tiles // group,),
        out_shape=[
            jax.ShapeDtypeStruct(obs_x.shape, BF16),
            jax.ShapeDtypeStruct(obs_x.shape, BF16),
            jax.ShapeDtypeStruct((own_rows, 2 * attn), F32),
            jax.ShapeDtypeStruct((2 * edge, 2 * attn), BF16),
            jax.ShapeDtypeStruct((n_lon, rows, attn), BF16),
        ],
        in_specs=[
            smem, smem, tile_spec, tile_spec, whole(n_tiles, length), whole(own_rows, width),
            whole(edge, width), whole(edge, width), whole(width, attn), whole(width, attn),
            whole(width, attn), whole(attn, width),
        ],
        out_specs=[
            tile_spec, tile_spec, whole(own_rows, 2 * attn), whole(2 * edge, 2 * attn),
            whole(n_lon, rows, attn),
        ],
        scratch_shapes=[
            pltpu.VMEM((wide + SUB, attn), F32),
            pltpu.VMEM((wide + SUB, attn), F32),
            pltpu.VMEM((wide + SUB, attn), F32),
            pltpu.VMEM((wide + SUB, attn), F32),
            pltpu.VMEM((width, attn), F32),
            pltpu.VMEM((attn, width), F32),
        ],
        name="attend",
    )(tile_window, band_counts, obs_x, obs_cot, point_mask, flat, low, high,
      w_query, w_key, w_value, w_out)

    latent_grad, query_grad, key_grad, value_grad, out_grad = pl.pallas_call(
        functools.partial(reduce_kernel, n_inst, n_lon),
        out_shape=[
            jax.ShapeDtypeStruct((own_rows, width), F32),
            jax.ShapeDtypeStruct((width, attn), F32),
            jax.ShapeDtypeStruct((width, attn), F32),
            jax.ShapeDtypeStruct((width, attn), F32),
            jax.ShapeDtypeStruct((attn, width), F32),
        ],
        in_specs=[vmem()] * 5,
        out_specs=[vmem()] * 5,
        scratch_shapes=[
            pltpu.VMEM((2, edge, 2 * attn), BF16),
            pltpu.VMEM((n_inst, own_rows, 2 * attn), BF16),
            pltpu.VMEM((n_lon, rows, attn), BF16),
            pltpu.VMEM((n_inst, rows, attn), F32),
            pltpu.VMEM((n_lon, rows, attn), BF16),
            dma((2,)), dma((2,)),
            dma((n_inst,)), dma((n_inst,)),
            dma((n_lon,)), dma((n_lon,)),
            dma((n_inst,)), dma((n_inst,)),
            dma((n_lon,)), dma((n_lon,)),
        ],
        compiler_params=pltpu.CompilerParams(collective_id=1, has_side_effects=True),
        name="reduce",
    )(own, halo, g, w_key, w_value)
    return (
        decoded,
        obs_grad,
        latent_grad.reshape(band_cols, lat_rows, width),
        query_grad,
        key_grad,
        value_grad,
        out_grad,
    )


def solution(mesh):
    placed = (
        P(("inst", "lon"), None, None),
        P(("inst", "lon"), None, None),
        P(("inst", "lon"), None),
        P(("inst", "lon"), None),
        P(("inst", "lon")),
        P("lon", None, None),
        P(),
        P(),
        P(),
        P(),
    )
    return jax.shard_map(
        functools.partial(shards, mesh.shape["inst"], mesh.shape["lon"]),
        mesh=mesh,
        in_specs=placed,
        out_specs=(
            P(("inst", "lon"), None, None),
            P(("inst", "lon"), None, None),
            P("lon", None, None),
            P(),
            P(),
            P(),
            P(),
        ),
        check_vma=False,
    )
```

```python
import functools
import math

import jax
import jax.numpy as jnp
from jax import lax
from jax.experimental import pallas as pl
from jax.experimental.pallas import tpu as pltpu
from jax.sharding import PartitionSpec as P

HEADS = 4
REACH = 2
WINDOW = 2 * REACH + 1
SUB = 8
CAP = 30.0
MESH = pl.DeviceIdType.MESH
F32 = jnp.float32
BF16 = jnp.bfloat16

NT = (((1,), (1,)), ((), ()))
TN = (((0,), (0,)), ((), ()))


def dot(a, b, dims=(((1,), (0,)), ((), ()))):
    return lax.dot_general(a, b, dims, preferred_element_type=F32)


def send(src, dst, send_sem, recv_sem, target):
    copy = pltpu.make_async_remote_copy(
        src_ref=src, dst_ref=dst, send_sem=send_sem, recv_sem=recv_sem, device_id=target,
        device_id_type=MESH)
    copy.start()
    return copy


def halo_kernel(n_inst, n_lon, parts, lat, low, high, send_sem, recv_sem, fan_send, fan_recv):
    me, mi = lax.axis_index("lon"), lax.axis_index("inst")
    right, left = lax.rem(me + 1, n_lon), lax.rem(me + n_lon - 1, n_lon)
    peers = [lax.rem(mi + d, n_inst) for d in range(1, n_inst)] if parts > 1 else []
    barrier = pltpu.get_barrier_semaphore()
    for other in (left, right):
        pl.semaphore_signal(barrier, inc=1, device_id={"lon": other}, device_id_type=MESH)
    for other in peers:
        pl.semaphore_signal(barrier, inc=1, device_id={"inst": other}, device_id_type=MESH)
    pl.semaphore_wait(barrier, 2 + len(peers))
    mine = mi if parts > 1 else 0
    first = send(lat.at[parts + mine], low.at[mine], send_sem.at[0], recv_sem.at[0], {"lon": right})
    second = send(lat.at[mine], high.at[mine], send_sem.at[1], recv_sem.at[1], {"lon": left})
    fans = []
    for side, (copy, block) in enumerate(((first, low), (second, high))):
        copy.wait_recv()
        for d, other in enumerate(peers):
            fans.append(send(
                block.at[mine], block.at[mine], fan_send.at[side, d], fan_recv.at[side, d],
                {"inst": other}))
    first.wait_send()
    second.wait_send()
    for copy in fans:
        copy.wait()


def attend_kernel(
    lon_cols, lat_rows, tw, cnt, x_ref, cot_ref, mask_ref, lat, low, high, wq, wk, wv, wo,
    dec, og, own_out, halo_out, g_out, keys, values, kg, vg, qg, outg,
):
    step = pl.program_id(0)
    tiles, length, width = x_ref.shape
    attn = wq.shape[1]
    head = attn // HEADS
    scale = 1.0 / math.sqrt(head)
    own_rows, edge = lat.shape[0], low.shape[0]
    wide = own_rows + 2 * edge
    slots = WINDOW * SUB
    band_cols = own_rows // lat_rows

    @pl.when(step == 0)
    def _():
        w_pair = jnp.concatenate([wk[...], wv[...]], axis=1)

        def project(block):
            return dot(block[...], w_pair).astype(BF16).astype(F32)

        for ref, first, count in ((low, 0, edge), (lat, edge, own_rows), (high, edge + own_rows, edge)):
            block = project(ref)
            keys[pl.ds(first, count), :] = block[:, :attn]
            values[pl.ds(first, count), :] = block[:, attn:]
        keys[pl.ds(wide, SUB), :] = jnp.zeros((SUB, attn), F32)
        values[pl.ds(wide, SUB), :] = jnp.zeros((SUB, attn), F32)
        kg[...] = jnp.zeros_like(kg)
        vg[...] = jnp.zeros_like(vg)
        qg[...] = jnp.zeros_like(qg)
        outg[...] = jnp.zeros_like(outg)

    flat_x = x_ref[...].reshape(tiles * length, width)
    flat_cot = cot_ref[...].reshape(tiles * length, width)
    queries = dot(flat_x, wq[...]).astype(BF16)

    row_id = lax.broadcasted_iota(jnp.int32, (length, width), 0)
    lives = []
    for j in range(tiles):
        t = step * tiles + j
        used = jnp.sum(mask_ref[pl.ds(t, 1), :], axis=1, keepdims=True)
        used = jnp.where(t < cnt[0], used, 0)
        lives.append(row_id < used)
    live = jnp.concatenate([m.astype(F32) for m in lives], axis=0)
    masked = (flat_cot.astype(F32) * live).astype(BF16)
    att_grad = dot(masked, wo[...], NT).astype(BF16)

    lane = lax.broadcasted_iota(jnp.int32, (1, attn), 1) // head
    head_mask = [(lane == h).astype(F32) for h in range(HEADS)]
    slot_id = lax.broadcasted_iota(jnp.int32, (slots, length), 0)
    valid = ((slot_id & (SUB - 1)) < WINDOW)[None]
    band_first = lax.axis_index("lon") * band_cols

    att_parts, query_parts = [], []
    for j in range(tiles):
        t = step * tiles + j
        col = lax.rem(tw[0, t] - band_first + REACH + lon_cols, lon_cols)
        base = col * lat_rows + tw[1, t]
        q_t = queries[j * length : (j + 1) * length]
        g_t = att_grad[j * length : (j + 1) * length]
        spans = [pl.ds(base + a * lat_rows, SUB) for a in range(WINDOW)]
        kw = jnp.concatenate([keys[at, :] for at in spans], axis=0)
        vw = jnp.concatenate([values[at, :] for at in spans], axis=0)
        kb = jnp.concatenate([kw * m for m in head_mask], axis=0).astype(BF16)
        vb = jnp.concatenate([vw * m for m in head_mask], axis=0).astype(BF16)
        th = jnp.tanh(dot(kb, q_t, NT) * scale / CAP).reshape(HEADS, slots, length)
        e = jnp.where(valid, jnp.exp(CAP * th), 0.0)
        p = e * (1.0 / jnp.sum(e, axis=1, keepdims=True))
        dp = dot(vb, g_t, NT).reshape(HEADS, slots, length)
        inner = jnp.sum(p * dp, axis=1, keepdims=True)
        sg = p * (dp - inner) * (1.0 - th * th) * scale
        sg = sg.reshape(HEADS * slots, length).astype(BF16)
        pb = p.reshape(HEADS * slots, length).astype(BF16)
        att_parts.append(dot(pb, vb, TN).astype(BF16))
        query_parts.append(dot(sg, kb, TN).astype(BF16))
        kp = dot(sg, q_t)
        vp = dot(pb, g_t)
        k_sum = sum(kp[h * slots : (h + 1) * slots] * head_mask[h] for h in range(HEADS))
        v_sum = sum(vp[h * slots : (h + 1) * slots] * head_mask[h] for h in range(HEADS))
        for a, at in enumerate(spans):
            kg[at, :] = kg[at, :] + k_sum[a * SUB : (a + 1) * SUB]
            vg[at, :] = vg[at, :] + v_sum[a * SUB : (a + 1) * SUB]

    attended = jnp.concatenate(att_parts, axis=0)
    query_part = jnp.concatenate(query_parts, axis=0)
    dec[...] = (flat_x.astype(F32) + live * dot(attended, wo[...])).astype(BF16).reshape(dec.shape)
    og[...] = (flat_cot.astype(F32) + dot(query_part, wq[...], NT)).astype(BF16).reshape(og.shape)
    qg[...] += dot(flat_x, query_part, TN)
    outg[...] += dot(attended, masked, TN)

    @pl.when(step == pl.num_programs(0) - 1)
    def _():
        half = own_out.shape[1]
        parts = own_out.shape[0] // 2
        for ref, lanes in ((kg, pl.ds(0, attn)), (vg, pl.ds(attn, attn))):
            for k in range(2 * parts):
                own_out[k, :, lanes] = ref[pl.ds(edge + k * half, half), :]
                at = k * half if k < parts else own_rows + k * half
                halo_out[k, :, lanes] = ref[pl.ds(at, half), :].astype(BF16)
        kv = jnp.zeros((width, 2 * attn), F32)
        for ref, first, count in ((low, 0, edge), (lat, edge, own_rows), (high, edge + own_rows, edge)):
            rows_at = pl.ds(first, count)
            grad = jnp.concatenate([kg[rows_at, :], vg[rows_at, :]], axis=1)
            grad_high = grad.astype(BF16)
            grad_low = (grad - grad_high.astype(F32)).astype(BF16)
            kv = kv + dot(ref[...], grad_high, TN) + dot(ref[...], grad_low, TN)
        rows = g_out.shape[1]
        pieces = (qg[...], kv[:, :attn], kv[:, attn:], outg[:, :attn], outg[:, attn:])
        at = 0
        for piece in pieces:
            count = piece.shape[0] // rows
            g_out[pl.ds(at, count)] = piece.astype(BF16).reshape(count, rows, attn)
            at += count


def reduce_kernel(
    n_inst, n_lon, parts, own, halo, g, shares, ag,
    pre, hsum, hbuf, share, rs, part, mine, b_s, b_r, h_s, h_r, i_s, i_r, rs_s, rs_r,
    p_s, p_r, a_s, a_r, local,
):
    me, mi = lax.axis_index("lon"), lax.axis_index("inst")
    slot = mi if parts > 1 else 0

    def lon_at(d):
        return lax.rem(me + d, n_lon)

    def inst_at(d):
        return lax.rem(mi + d, n_inst)

    barrier = pltpu.get_barrier_semaphore()
    for d in range(1, n_lon):
        pl.semaphore_signal(barrier, inc=1, device_id={"lon": lon_at(d)}, device_id_type=MESH)
    for d in range(1, n_inst):
        pl.semaphore_signal(barrier, inc=1, device_id={"inst": inst_at(d)}, device_id_type=MESH)
    pl.semaphore_wait(barrier, n_lon + n_inst - 2)

    joined = []
    if parts > 1:
        for side in range(2):
            for d in range(1, n_inst):
                joined.append(send(
                    halo.at[side * parts + inst_at(d)], pre.at[side, d], b_s.at[side, d],
                    b_r.at[side, d], {"inst": inst_at(d)}))
    scatters = [
        send(g.at[lon_at(d)], rs.at[d], rs_s.at[d], rs_r.at[d], {"lon": lon_at(d)})
        for d in range(1, n_lon)
    ]
    for k in range(2 * parts):
        share[k] = own[k].astype(BF16)
    for copy in joined:
        copy.wait()
    halos = []
    for side, d in ((0, n_lon - 1), (1, 1)):
        total = halo[side * parts + slot].astype(F32)
        if parts > 1:
            for e in range(1, n_inst):
                total = total + pre[side, e].astype(F32)
        hsum[side] = total.astype(BF16)
        halos.append(send(
            hsum.at[side], hbuf.at[side], h_s.at[side], h_r.at[side], {"lon": lon_at(d)}))
    for copy in scatters:
        copy.wait()
    total = g[me].astype(F32)
    for d in range(1, n_lon):
        total = total + rs[d].astype(F32)
    part[mi] = total
    swaps = [
        send(part.at[mi], part.at[mi], p_s.at[d], p_r.at[d], {"inst": inst_at(d)})
        for d in range(1, n_inst)
    ]
    for copy in swaps:
        copy.wait()
    total = part[0]
    for i in range(1, n_inst):
        total = total + part[i]
    mine[...] = total.astype(BF16)
    gathers = [
        send(mine, ag.at[me], a_s.at[d], a_r.at[d], {"lon": lon_at(d)})
        for d in range(1, n_lon)
    ]
    gathers.append(pltpu.make_async_copy(mine, ag.at[me], local.at[0]))
    gathers[-1].start()
    for copy in halos:
        copy.wait()
    share[slot] = (own[slot] + hbuf[1].astype(F32)).astype(BF16)
    share[parts + slot] = (own[parts + slot] + hbuf[0].astype(F32)).astype(BF16)
    joins = [
        send(share, shares.at[mi], i_s.at[d], i_r.at[d], {"inst": inst_at(d)})
        for d in range(1, n_inst)
    ]
    joins.append(pltpu.make_async_copy(share, shares.at[mi], local.at[1]))
    joins[-1].start()
    for copy in joins:
        copy.wait()
    for copy in gathers:
        copy.wait()


def finish_kernel(shares, ag, wk, wv, lat_out, q_out, k_out, v_out, o_out):
    attn = wk.shape[1]
    grad = shares[0, 0].astype(F32)
    for i in range(1, shares.shape[0]):
        grad = grad + shares[i, 0].astype(F32)
    grad_high = grad.astype(BF16)
    grad_low = (grad - grad_high.astype(F32)).astype(BF16)
    w_pair = jnp.concatenate([wk[...], wv[...]], axis=1)
    lat_out[...] = dot(grad_high, w_pair, NT) + dot(grad_low, w_pair, NT)

    @pl.when(pl.program_id(0) == 0)
    def _():
        rows = ag.shape[1]
        at = 0
        out_parts = [o_out.at[:, pl.ds(0, attn)], o_out.at[:, pl.ds(attn, attn)]]
        for out in [q_out, k_out, v_out] + out_parts:
            count = out.shape[0] // rows
            out[...] = ag[pl.ds(at, count)].astype(F32).reshape(out.shape)
            at += count


def vmem():
    return pl.BlockSpec(memory_space=pltpu.VMEM)


def shards(
    n_inst, n_lon, obs_x, obs_cot, tile_window, point_mask, band_counts, latents,
    w_query, w_key, w_value, w_out,
):
    n_tiles, length, width = obs_x.shape
    band_cols, lat_rows, _ = latents.shape
    attn = w_query.shape[1]
    edge, own_rows = REACH * lat_rows, band_cols * lat_rows
    wide = own_rows + 2 * edge
    flat = latents.reshape(own_rows, width)
    parts = n_inst if edge % (SUB * n_inst) == 0 else 1
    half = edge // parts
    dma = pltpu.SemaphoreType.DMA
    anywhere = pl.BlockSpec(memory_space=pl.ANY)
    low, high = pl.pallas_call(
        functools.partial(halo_kernel, n_inst, n_lon, parts),
        out_shape=[jax.ShapeDtypeStruct((parts, half, width), BF16)] * 2,
        in_specs=[anywhere],
        out_specs=[anywhere] * 2,
        scratch_shapes=[dma((2,)), dma((2,)), dma((2, n_inst)), dma((2, n_inst))],
        compiler_params=pltpu.CompilerParams(collective_id=0, has_side_effects=True),
        name="halo",
    )(latents.reshape(2 * parts, half, width))
    low, high = low.reshape(edge, width), high.reshape(edge, width)

    group = next(b for b in (4, 3, 2, 1) if n_tiles % b == 0)
    weight_rows = 2 * width + 2 * attn + width
    rows = weight_rows // n_lon
    whole = lambda *shape: pl.BlockSpec(shape, lambda i: (0,) * len(shape))
    tile_spec = pl.BlockSpec((group, length, width), lambda i: (i, 0, 0))
    smem = pl.BlockSpec(memory_space=pltpu.SMEM)
    decoded, obs_grad, own, halo, g = pl.pallas_call(
        functools.partial(attend_kernel, band_cols * n_lon, lat_rows),
        grid=(n_tiles // group,),
        out_shape=[
            jax.ShapeDtypeStruct(obs_x.shape, BF16),
            jax.ShapeDtypeStruct(obs_x.shape, BF16),
            jax.ShapeDtypeStruct((2 * parts, half, 2 * attn), F32),
            jax.ShapeDtypeStruct((2 * parts, half, 2 * attn), BF16),
            jax.ShapeDtypeStruct((n_lon, rows, attn), BF16),
        ],
        in_specs=[
            smem, smem, tile_spec, tile_spec, whole(n_tiles, length), whole(own_rows, width),
            whole(edge, width), whole(edge, width), whole(width, attn), whole(width, attn),
            whole(width, attn), whole(attn, width),
        ],
        out_specs=[
            tile_spec, tile_spec, whole(2 * parts, half, 2 * attn), whole(2 * parts, half, 2 * attn),
            whole(n_lon, rows, attn),
        ],
        scratch_shapes=[
            pltpu.VMEM((wide + SUB, attn), F32),
            pltpu.VMEM((wide + SUB, attn), F32),
            pltpu.VMEM((wide + SUB, attn), F32),
            pltpu.VMEM((wide + SUB, attn), F32),
            pltpu.VMEM((width, attn), F32),
            pltpu.VMEM((attn, width), F32),
        ],
        name="attend",
    )(tile_window.T, band_counts, obs_x, obs_cot, point_mask, flat, low, high,
      w_query, w_key, w_value, w_out)

    shares, ag = pl.pallas_call(
        functools.partial(reduce_kernel, n_inst, n_lon, parts),
        out_shape=[
            jax.ShapeDtypeStruct((n_inst, 2 * parts, half, 2 * attn), BF16),
            jax.ShapeDtypeStruct((n_lon, rows, attn), BF16),
        ],
        in_specs=[vmem()] * 3,
        out_specs=[anywhere] * 2,
        scratch_shapes=[
            pltpu.VMEM((2, n_inst, half, 2 * attn), BF16),
            pltpu.VMEM((2, half, 2 * attn), BF16),
            pltpu.VMEM((2, half, 2 * attn), BF16),
            pltpu.VMEM((2 * parts, half, 2 * attn), BF16),
            pltpu.VMEM((n_lon, rows, attn), BF16),
            pltpu.VMEM((n_inst, rows, attn), F32),
            pltpu.VMEM((rows, attn), BF16),
            dma((2, n_inst)), dma((2, n_inst)),
            dma((2,)), dma((2,)),
            dma((n_inst,)), dma((n_inst,)),
            dma((n_lon,)), dma((n_lon,)),
            dma((n_inst,)), dma((n_inst,)),
            dma((n_lon,)), dma((n_lon,)),
            dma((2,)),
        ],
        compiler_params=pltpu.CompilerParams(collective_id=1, has_side_effects=True),
        name="reduce",
    )(own, halo, g)
    latent_grad, query_grad, key_grad, value_grad, out_grad = pl.pallas_call(
        finish_kernel,
        grid=(2 * parts,),
        out_shape=[
            jax.ShapeDtypeStruct((own_rows, width), F32),
            jax.ShapeDtypeStruct((width, attn), F32),
            jax.ShapeDtypeStruct((width, attn), F32),
            jax.ShapeDtypeStruct((width, attn), F32),
            jax.ShapeDtypeStruct((attn, width), F32),
        ],
        in_specs=[
            pl.BlockSpec((n_inst, 1, half, 2 * attn), lambda i: (0, i, 0, 0)),
            whole(n_lon, rows, attn), whole(width, attn), whole(width, attn),
        ],
        out_specs=[
            pl.BlockSpec((half, width), lambda i: (i, 0)), whole(width, attn),
            whole(width, attn), whole(width, attn), whole(attn, width),
        ],
        name="finish",
    )(shares, ag, w_key, w_value)
    return (
        decoded,
        obs_grad,
        latent_grad.reshape(band_cols, lat_rows, width),
        query_grad,
        key_grad,
        value_grad,
        out_grad,
    )


def solution(mesh):
    placed = (
        P(("inst", "lon"), None, None),
        P(("inst", "lon"), None, None),
        P(("inst", "lon"), None),
        P(("inst", "lon"), None),
        P(("inst", "lon")),
        P("lon", None, None),
        P(),
        P(),
        P(),
        P(),
    )
    return jax.shard_map(
        functools.partial(shards, mesh.shape["inst"], mesh.shape["lon"]),
        mesh=mesh,
        in_specs=placed,
        out_specs=(
            P(("inst", "lon"), None, None),
            P(("inst", "lon"), None, None),
            P("lon", None, None),
            P(),
            P(),
            P(),
            P(),
        ),
        check_vma=False,
    )
```

```python
import functools
import math

import jax
import jax.numpy as jnp
from jax import lax
from jax.experimental import pallas as pl
from jax.experimental.pallas import tpu as pltpu
from jax.sharding import PartitionSpec as P

HEADS = 4
REACH = 2
WINDOW = 2 * REACH + 1
SUB = 8
CAP = 30.0
MESH = pl.DeviceIdType.MESH
F32 = jnp.float32
BF16 = jnp.bfloat16

NT = (((1,), (1,)), ((), ()))
TN = (((0,), (0,)), ((), ()))


def dot(a, b, dims=(((1,), (0,)), ((), ()))):
    return lax.dot_general(a, b, dims, preferred_element_type=F32)


def send(src, dst, send_sem, recv_sem, target):
    copy = pltpu.make_async_remote_copy(
        src_ref=src, dst_ref=dst, send_sem=send_sem, recv_sem=recv_sem, device_id=target,
        device_id_type=MESH)
    copy.start()
    return copy


def live_rows(mask_ref, cnt, first, tiles, width):
    length = mask_ref.shape[1]
    row_id = lax.broadcasted_iota(jnp.int32, (length, width), 0)
    blocks = []
    for j in range(tiles):
        t = first + j
        used = jnp.sum(mask_ref[pl.ds(t, 1), :], axis=1, keepdims=True)
        used = jnp.where(t < cnt[0], used, 0)
        blocks.append((row_id < used).astype(F32))
    return jnp.concatenate(blocks, axis=0)


def halo_kernel(
    n_inst, n_lon, parts, group, lat, x_hbm, cot_hbm, mask_ref, cnt, wq, wo,
    low, high, q_hbm, g_hbm, x_ref, cot_ref, q_ref, g_ref,
    send_sem, recv_sem, fan_send, fan_recv, load, store,
):
    loads = [pltpu.make_async_copy(x_hbm, x_ref, load.at[0]),
             pltpu.make_async_copy(cot_hbm, cot_ref, load.at[1])]
    for copy in loads:
        copy.start()
    me, mi = lax.axis_index("lon"), lax.axis_index("inst")
    right, left = lax.rem(me + 1, n_lon), lax.rem(me + n_lon - 1, n_lon)
    peers = [lax.rem(mi + d, n_inst) for d in range(1, n_inst)] if parts > 1 else []
    barrier = pltpu.get_barrier_semaphore()
    for other in (left, right):
        pl.semaphore_signal(barrier, inc=1, device_id={"lon": other}, device_id_type=MESH)
    for other in peers:
        pl.semaphore_signal(barrier, inc=1, device_id={"inst": other}, device_id_type=MESH)
    pl.semaphore_wait(barrier, 2 + len(peers))
    mine = mi if parts > 1 else 0
    first = send(lat.at[parts + mine], low.at[mine], send_sem.at[0], recv_sem.at[0], {"lon": right})
    second = send(lat.at[mine], high.at[mine], send_sem.at[1], recv_sem.at[1], {"lon": left})
    for copy in loads:
        copy.wait()
    n_tiles, length, width = x_ref.shape
    for k in range(0, n_tiles, group):
        at = pl.ds(k, group)
        shape = (group, length, q_ref.shape[2])
        flat = x_ref[at].reshape(group * length, width)
        q_ref[at] = dot(flat, wq[...]).astype(BF16).reshape(shape)
        live = live_rows(mask_ref, cnt, k, group, width)
        masked = (cot_ref[at].reshape(group * length, width).astype(F32) * live).astype(BF16)
        g_ref[at] = dot(masked, wo[...], NT).astype(BF16).reshape(shape)
    stores = [pltpu.make_async_copy(q_ref, q_hbm, store.at[0]),
              pltpu.make_async_copy(g_ref, g_hbm, store.at[1])]
    for copy in stores:
        copy.start()
    fans = []
    for side, (copy, block) in enumerate(((first, low), (second, high))):
        copy.wait_recv()
        for d, other in enumerate(peers):
            fans.append(send(
                block.at[mine], block.at[mine], fan_send.at[side, d], fan_recv.at[side, d],
                {"inst": other}))
    first.wait_send()
    second.wait_send()
    for copy in fans + stores:
        copy.wait()


def attend_kernel(
    lon_cols, lat_rows, tw, cnt, x_ref, cot_ref, q_ref, g_ref, mask_ref, lat, low, high, wq, wk, wv, wo,
    dec, og, own_out, halo_out, g_out, keys, values, kg, vg, qg, outg,
):
    step = pl.program_id(0)
    tiles, length, width = x_ref.shape
    attn = wq.shape[1]
    head = attn // HEADS
    scale = 1.0 / math.sqrt(head)
    own_rows, edge = lat.shape[0], low.shape[0]
    wide = own_rows + 2 * edge
    slots = WINDOW * SUB
    band_cols = own_rows // lat_rows

    @pl.when(step == 0)
    def _():
        w_pair = jnp.concatenate([wk[...], wv[...]], axis=1)

        def project(block):
            return dot(block[...], w_pair).astype(BF16).astype(F32)

        for ref, first, count in ((low, 0, edge), (lat, edge, own_rows), (high, edge + own_rows, edge)):
            block = project(ref)
            keys[pl.ds(first, count), :] = block[:, :attn]
            values[pl.ds(first, count), :] = block[:, attn:]
        keys[pl.ds(wide, SUB), :] = jnp.zeros((SUB, attn), F32)
        values[pl.ds(wide, SUB), :] = jnp.zeros((SUB, attn), F32)
        kg[...] = jnp.zeros_like(kg)
        vg[...] = jnp.zeros_like(vg)
        qg[...] = jnp.zeros_like(qg)
        outg[...] = jnp.zeros_like(outg)

    flat_x = x_ref[...].reshape(tiles * length, width)
    flat_cot = cot_ref[...].reshape(tiles * length, width)
    live = live_rows(mask_ref, cnt, step * tiles, tiles, width)
    masked = (flat_cot.astype(F32) * live).astype(BF16)

    lane = lax.broadcasted_iota(jnp.int32, (1, attn), 1) // head
    head_mask = [(lane == h).astype(F32) for h in range(HEADS)]
    slot_id = lax.broadcasted_iota(jnp.int32, (slots, length), 0)
    valid = ((slot_id & (SUB - 1)) < WINDOW)[None]
    band_first = lax.axis_index("lon") * band_cols

    att_parts, query_parts = [], []
    for j in range(tiles):
        t = step * tiles + j
        col = lax.rem(tw[0, t] - band_first + REACH + lon_cols, lon_cols)
        base = col * lat_rows + tw[1, t]
        q_t = q_ref[j]
        g_t = g_ref[j]
        spans = [pl.ds(base + a * lat_rows, SUB) for a in range(WINDOW)]
        kw = jnp.concatenate([keys[at, :] for at in spans], axis=0)
        vw = jnp.concatenate([values[at, :] for at in spans], axis=0)
        kb = jnp.concatenate([kw * m for m in head_mask], axis=0).astype(BF16)
        vb = jnp.concatenate([vw * m for m in head_mask], axis=0).astype(BF16)
        th = jnp.tanh(dot(kb, q_t, NT) * scale / CAP).reshape(HEADS, slots, length)
        e = jnp.where(valid, jnp.exp(CAP * th), 0.0)
        p = e * (1.0 / jnp.sum(e, axis=1, keepdims=True))
        dp = dot(vb, g_t, NT).reshape(HEADS, slots, length)
        inner = jnp.sum(p * dp, axis=1, keepdims=True)
        sg = p * (dp - inner) * (1.0 - th * th) * scale
        sg = sg.reshape(HEADS * slots, length).astype(BF16)
        pb = p.reshape(HEADS * slots, length).astype(BF16)
        att_parts.append(dot(pb, vb, TN).astype(BF16))
        query_parts.append(dot(sg, kb, TN).astype(BF16))
        kp = dot(sg, q_t)
        vp = dot(pb, g_t)
        k_sum = sum(kp[h * slots : (h + 1) * slots] * head_mask[h] for h in range(HEADS))
        v_sum = sum(vp[h * slots : (h + 1) * slots] * head_mask[h] for h in range(HEADS))
        for a, at in enumerate(spans):
            kg[at, :] = kg[at, :] + k_sum[a * SUB : (a + 1) * SUB]
            vg[at, :] = vg[at, :] + v_sum[a * SUB : (a + 1) * SUB]

    attended = jnp.concatenate(att_parts, axis=0)
    query_part = jnp.concatenate(query_parts, axis=0)
    dec[...] = (flat_x.astype(F32) + live * dot(attended, wo[...])).astype(BF16).reshape(dec.shape)
    og[...] = (flat_cot.astype(F32) + dot(query_part, wq[...], NT)).astype(BF16).reshape(og.shape)
    qg[...] += dot(flat_x, query_part, TN)
    outg[...] += dot(attended, masked, TN)

    @pl.when(step == pl.num_programs(0) - 1)
    def _():
        half = own_out.shape[1]
        parts = own_out.shape[0] // 2
        for ref, lanes in ((kg, pl.ds(0, attn)), (vg, pl.ds(attn, attn))):
            for k in range(2 * parts):
                own_out[k, :, lanes] = ref[pl.ds(edge + k * half, half), :]
                at = k * half if k < parts else own_rows + k * half
                halo_out[k, :, lanes] = ref[pl.ds(at, half), :].astype(BF16)
        kv = jnp.zeros((width, 2 * attn), F32)
        for ref, first, count in ((low, 0, edge), (lat, edge, own_rows), (high, edge + own_rows, edge)):
            rows_at = pl.ds(first, count)
            grad = jnp.concatenate([kg[rows_at, :], vg[rows_at, :]], axis=1)
            grad_high = grad.astype(BF16)
            grad_low = (grad - grad_high.astype(F32)).astype(BF16)
            kv = kv + dot(ref[...], grad_high, TN) + dot(ref[...], grad_low, TN)
        rows = g_out.shape[1]
        pieces = (qg[...], kv[:, :attn], kv[:, attn:], outg[:, :attn], outg[:, attn:])
        at = 0
        for piece in pieces:
            count = piece.shape[0] // rows
            g_out[pl.ds(at, count)] = piece.astype(BF16).reshape(count, rows, attn)
            at += count


def reduce_kernel(
    n_inst, n_lon, parts, gp, own, halo, g, shares, ag,
    pre, hsum, hbuf, share, rs, part, mine, gpre, gsum, b_s, b_r, h_s, h_r, i_s, i_r, rs_s, rs_r,
    p_s, p_r, a_s, a_r, f_s, f_r, local,
):
    me, mi = lax.axis_index("lon"), lax.axis_index("inst")
    slot = mi if parts > 1 else 0

    def lon_at(d):
        return lax.rem(me + d, n_lon)

    def inst_at(d):
        return lax.rem(mi + d, n_inst)

    barrier = pltpu.get_barrier_semaphore()
    for d in range(1, n_lon):
        pl.semaphore_signal(barrier, inc=1, device_id={"lon": lon_at(d)}, device_id_type=MESH)
    for d in range(1, n_inst):
        pl.semaphore_signal(barrier, inc=1, device_id={"inst": inst_at(d)}, device_id_type=MESH)
    pl.semaphore_wait(barrier, n_lon + n_inst - 2)

    joined, presums = [], []
    if gp > 1:
        presums = [
            send(g.at[pl.ds(inst_at(d) * n_lon, n_lon)], gpre.at[d], p_s.at[d], p_r.at[d],
                 {"inst": inst_at(d)})
            for d in range(1, n_inst)
        ]
    if parts > 1:
        for side in range(2):
            for d in range(1, n_inst):
                joined.append(send(
                    halo.at[side * parts + inst_at(d)], pre.at[side, d], b_s.at[side, d],
                    b_r.at[side, d], {"inst": inst_at(d)}))
    if gp > 1:
        for copy in presums:
            copy.wait()
        total = g[pl.ds(mi * n_lon, n_lon)].astype(F32)
        for d in range(1, n_inst):
            total = total + gpre[d].astype(F32)
        gsum[...] = total.astype(BF16)
        source = gsum
    else:
        source = g
    scatters = [
        send(source.at[lon_at(d)], rs.at[d], rs_s.at[d], rs_r.at[d], {"lon": lon_at(d)})
        for d in range(1, n_lon)
    ]
    for copy in joined:
        copy.wait()
    halos = []
    for side, d in ((0, n_lon - 1), (1, 1)):
        total = halo[side * parts + slot].astype(F32)
        if parts > 1:
            for e in range(1, n_inst):
                total = total + pre[side, e].astype(F32)
        hsum[side] = total.astype(BF16)
        halos.append(send(
            hsum.at[side], hbuf.at[side], h_s.at[side], h_r.at[side], {"lon": lon_at(d)}))
    for k in range(2 * parts):
        share[k] = own[k].astype(BF16)
    for copy in scatters:
        copy.wait()
    total = source[me].astype(F32)
    for d in range(1, n_lon):
        total = total + rs[d].astype(F32)
    if gp == 1:
        part[mi] = total
        swaps = [
            send(part.at[mi], part.at[mi], p_s.at[d], p_r.at[d], {"inst": inst_at(d)})
            for d in range(1, n_inst)
        ]
        for copy in swaps:
            copy.wait()
        total = part[0]
        for i in range(1, n_inst):
            total = total + part[i]
    mine[...] = total.astype(BF16)
    base = mi * n_lon if gp > 1 else 0
    gathers = [
        send(mine, ag.at[base + me], a_s.at[d], a_r.at[d], {"lon": lon_at(d)})
        for d in range(1, n_lon)
    ]
    fans = []
    if gp > 1:
        fans = [
            send(mine, ag.at[base + me], f_s.at[d, 0], f_r.at[d, 0], {"inst": inst_at(d)})
            for d in range(1, n_inst)
        ]
    keep = pltpu.make_async_copy(mine, ag.at[base + me], local.at[0])
    keep.start()
    for copy in halos:
        copy.wait()
    share[slot] = (own[slot] + hbuf[1].astype(F32)).astype(BF16)
    share[parts + slot] = (own[parts + slot] + hbuf[0].astype(F32)).astype(BF16)
    joins = [
        send(share, shares.at[mi], i_s.at[d], i_r.at[d], {"inst": inst_at(d)})
        for d in range(1, n_inst)
    ]
    joins.append(pltpu.make_async_copy(share, shares.at[mi], local.at[1]))
    joins[-1].start()
    for e, copy in enumerate(gathers, 1):
        copy.wait_recv()
        if gp > 1:
            at = base + lon_at(n_lon - e)
            for d in range(1, n_inst):
                fans.append(send(
                    ag.at[at], ag.at[at], f_s.at[d, e], f_r.at[d, e], {"inst": inst_at(d)}))
    for copy in gathers:
        copy.wait_send()
    for copy in joins + fans + [keep]:
        copy.wait()


def finish_kernel(shares, ag, wk, wv, lat_out, q_out, k_out, v_out, o_out):
    attn = wk.shape[1]
    grad = shares[0, 0].astype(F32)
    for i in range(1, shares.shape[0]):
        grad = grad + shares[i, 0].astype(F32)
    grad_high = grad.astype(BF16)
    grad_low = (grad - grad_high.astype(F32)).astype(BF16)
    w_pair = jnp.concatenate([wk[...], wv[...]], axis=1)
    lat_out[...] = dot(grad_high, w_pair, NT) + dot(grad_low, w_pair, NT)

    @pl.when(pl.program_id(0) == 0)
    def _():
        rows = ag.shape[1]
        at = 0
        out_parts = [o_out.at[:, pl.ds(0, attn)], o_out.at[:, pl.ds(attn, attn)]]
        for out in [q_out, k_out, v_out] + out_parts:
            count = out.shape[0] // rows
            out[...] = ag[pl.ds(at, count)].astype(F32).reshape(out.shape)
            at += count


def vmem():
    return pl.BlockSpec(memory_space=pltpu.VMEM)


def shards(
    n_inst, n_lon, obs_x, obs_cot, tile_window, point_mask, band_counts, latents,
    w_query, w_key, w_value, w_out,
):
    n_tiles, length, width = obs_x.shape
    band_cols, lat_rows, _ = latents.shape
    attn = w_query.shape[1]
    edge, own_rows = REACH * lat_rows, band_cols * lat_rows
    wide = own_rows + 2 * edge
    flat = latents.reshape(own_rows, width)
    parts = n_inst if edge % (SUB * n_inst) == 0 else 1
    half = edge // parts
    dma = pltpu.SemaphoreType.DMA
    anywhere = pl.BlockSpec(memory_space=pl.ANY)
    group = next(b for b in (4, 3, 2, 1) if n_tiles % b == 0)
    smem = pl.BlockSpec(memory_space=pltpu.SMEM)
    low, high, queries, att_grad = pl.pallas_call(
        functools.partial(halo_kernel, n_inst, n_lon, parts, group),
        out_shape=[jax.ShapeDtypeStruct((parts, half, width), BF16)] * 2
        + [jax.ShapeDtypeStruct((n_tiles, length, attn), BF16)] * 2,
        in_specs=[anywhere] * 3 + [vmem(), smem, vmem(), vmem()],
        out_specs=[anywhere] * 4,
        scratch_shapes=[
            pltpu.VMEM(obs_x.shape, BF16), pltpu.VMEM(obs_x.shape, BF16),
            pltpu.VMEM((n_tiles, length, attn), BF16), pltpu.VMEM((n_tiles, length, attn), BF16),
            dma((2,)), dma((2,)), dma((2, n_inst)), dma((2, n_inst)), dma((2,)), dma((2,)),
        ],
        compiler_params=pltpu.CompilerParams(collective_id=0, has_side_effects=True),
        name="halo",
    )(latents.reshape(2 * parts, half, width), obs_x, obs_cot, point_mask, band_counts,
      w_query, w_out)
    low, high = low.reshape(edge, width), high.reshape(edge, width)

    weight_rows = 2 * width + 2 * attn + width
    rows = weight_rows // n_lon
    gp = n_inst if rows % (2 * SUB * n_inst) == 0 else 1
    rows = rows // gp
    head_spec = pl.BlockSpec((group, length, attn), lambda i: (i, 0, 0))
    whole = lambda *shape: pl.BlockSpec(shape, lambda i: (0,) * len(shape))
    tile_spec = pl.BlockSpec((group, length, width), lambda i: (i, 0, 0))
    decoded, obs_grad, own, halo, g = pl.pallas_call(
        functools.partial(attend_kernel, band_cols * n_lon, lat_rows),
        grid=(n_tiles // group,),
        out_shape=[
            jax.ShapeDtypeStruct(obs_x.shape, BF16),
            jax.ShapeDtypeStruct(obs_x.shape, BF16),
            jax.ShapeDtypeStruct((2 * parts, half, 2 * attn), F32),
            jax.ShapeDtypeStruct((2 * parts, half, 2 * attn), BF16),
            jax.ShapeDtypeStruct((gp * n_lon, rows, attn), BF16),
        ],
        in_specs=[
            smem, smem, tile_spec, tile_spec, head_spec, head_spec, whole(n_tiles, length), whole(own_rows, width),
            whole(edge, width), whole(edge, width), whole(width, attn), whole(width, attn),
            whole(width, attn), whole(attn, width),
        ],
        out_specs=[
            tile_spec, tile_spec, whole(2 * parts, half, 2 * attn), whole(2 * parts, half, 2 * attn),
            whole(gp * n_lon, rows, attn),
        ],
        scratch_shapes=[
            pltpu.VMEM((wide + SUB, attn), F32),
            pltpu.VMEM((wide + SUB, attn), F32),
            pltpu.VMEM((wide + SUB, attn), F32),
            pltpu.VMEM((wide + SUB, attn), F32),
            pltpu.VMEM((width, attn), F32),
            pltpu.VMEM((attn, width), F32),
        ],
        name="attend",
    )(tile_window.T, band_counts, obs_x, obs_cot, queries, att_grad, point_mask, flat, low, high,
      w_query, w_key, w_value, w_out)

    shares, ag = pl.pallas_call(
        functools.partial(reduce_kernel, n_inst, n_lon, parts, gp),
        out_shape=[
            jax.ShapeDtypeStruct((n_inst, 2 * parts, half, 2 * attn), BF16),
            jax.ShapeDtypeStruct((gp * n_lon, rows, attn), BF16),
        ],
        in_specs=[vmem()] * 3,
        out_specs=[anywhere] * 2,
        scratch_shapes=[
            pltpu.VMEM((2, n_inst, half, 2 * attn), BF16),
            pltpu.VMEM((2, half, 2 * attn), BF16),
            pltpu.VMEM((2, half, 2 * attn), BF16),
            pltpu.VMEM((2 * parts, half, 2 * attn), BF16),
            pltpu.VMEM((n_lon, rows, attn), BF16),
            pltpu.VMEM((n_inst, rows, attn), F32),
            pltpu.VMEM((rows, attn), BF16),
            pltpu.VMEM((n_inst, n_lon, rows, attn), BF16),
            pltpu.VMEM((n_lon, rows, attn), BF16),
            dma((2, n_inst)), dma((2, n_inst)),
            dma((2,)), dma((2,)),
            dma((n_inst,)), dma((n_inst,)),
            dma((n_lon,)), dma((n_lon,)),
            dma((n_inst,)), dma((n_inst,)),
            dma((n_lon,)), dma((n_lon,)),
            dma((n_inst, n_lon)), dma((n_inst, n_lon)),
            dma((2,)),
        ],
        compiler_params=pltpu.CompilerParams(collective_id=1, has_side_effects=True),
        name="reduce",
    )(own, halo, g)
    latent_grad, query_grad, key_grad, value_grad, out_grad = pl.pallas_call(
        finish_kernel,
        grid=(2 * parts,),
        out_shape=[
            jax.ShapeDtypeStruct((own_rows, width), F32),
            jax.ShapeDtypeStruct((width, attn), F32),
            jax.ShapeDtypeStruct((width, attn), F32),
            jax.ShapeDtypeStruct((width, attn), F32),
            jax.ShapeDtypeStruct((attn, width), F32),
        ],
        in_specs=[
            pl.BlockSpec((n_inst, 1, half, 2 * attn), lambda i: (0, i, 0, 0)),
            whole(gp * n_lon, rows, attn), whole(width, attn), whole(width, attn),
        ],
        out_specs=[
            pl.BlockSpec((half, width), lambda i: (i, 0)), whole(width, attn),
            whole(width, attn), whole(width, attn), whole(attn, width),
        ],
        name="finish",
    )(shares, ag, w_key, w_value)
    return (
        decoded,
        obs_grad,
        latent_grad.reshape(band_cols, lat_rows, width),
        query_grad,
        key_grad,
        value_grad,
        out_grad,
    )


def solution(mesh):
    placed = (
        P(("inst", "lon"), None, None),
        P(("inst", "lon"), None, None),
        P(("inst", "lon"), None),
        P(("inst", "lon"), None),
        P(("inst", "lon")),
        P("lon", None, None),
        P(),
        P(),
        P(),
        P(),
    )
    return jax.shard_map(
        functools.partial(shards, mesh.shape["inst"], mesh.shape["lon"]),
        mesh=mesh,
        in_specs=placed,
        out_specs=(
            P(("inst", "lon"), None, None),
            P(("inst", "lon"), None, None),
            P("lon", None, None),
            P(),
            P(),
            P(),
            P(),
        ),
        check_vma=False,
    )
```

```python
import functools
import math

import jax
import jax.numpy as jnp
from jax import lax
from jax.experimental import pallas as pl
from jax.experimental.pallas import tpu as pltpu
from jax.sharding import PartitionSpec as P

HEADS = 4
REACH = 2
WINDOW = 2 * REACH + 1
SUB = 8
CAP = 30.0
MESH = pl.DeviceIdType.MESH
F32 = jnp.float32
BF16 = jnp.bfloat16

NT = (((1,), (1,)), ((), ()))
TN = (((0,), (0,)), ((), ()))


def dot(a, b, dims=(((1,), (0,)), ((), ()))):
    return lax.dot_general(a, b, dims, preferred_element_type=F32)


def send(src, dst, send_sem, recv_sem, target):
    copy = pltpu.make_async_remote_copy(
        src_ref=src, dst_ref=dst, send_sem=send_sem, recv_sem=recv_sem, device_id=target,
        device_id_type=MESH)
    copy.start()
    return copy


def halo_kernel(n_inst, n_lon, parts, lat, low, high, send_sem, recv_sem, fan_send, fan_recv):
    me, mi = lax.axis_index("lon"), lax.axis_index("inst")
    right, left = lax.rem(me + 1, n_lon), lax.rem(me + n_lon - 1, n_lon)
    peers = [lax.rem(mi + d, n_inst) for d in range(1, n_inst)] if parts > 1 else []
    barrier = pltpu.get_barrier_semaphore()
    for other in (left, right):
        pl.semaphore_signal(barrier, inc=1, device_id={"lon": other}, device_id_type=MESH)
    for other in peers:
        pl.semaphore_signal(barrier, inc=1, device_id={"inst": other}, device_id_type=MESH)
    pl.semaphore_wait(barrier, 2 + len(peers))
    mine = mi if parts > 1 else 0
    first = send(lat.at[parts + mine], low.at[mine], send_sem.at[0], recv_sem.at[0], {"lon": right})
    second = send(lat.at[mine], high.at[mine], send_sem.at[1], recv_sem.at[1], {"lon": left})
    fans = []
    for side, (copy, block) in enumerate(((first, low), (second, high))):
        copy.wait_recv()
        for d, other in enumerate(peers):
            fans.append(send(
                block.at[mine], block.at[mine], fan_send.at[side, d], fan_recv.at[side, d],
                {"inst": other}))
    first.wait_send()
    second.wait_send()
    for copy in fans:
        copy.wait()


def attend_kernel(
    lon_cols, lat_rows, tw, cnt, x_ref, cot_ref, mask_ref, lat, low, high, wq, wk, wv, wo,
    dec, og, own_out, halo_out, g_out, keys, values, kg, vg, qg, outg,
):
    step = pl.program_id(0)
    tiles, length, width = x_ref.shape
    attn = wq.shape[1]
    head = attn // HEADS
    scale = 1.0 / math.sqrt(head)
    own_rows, edge = lat.shape[0], low.shape[0]
    wide = own_rows + 2 * edge
    slots = WINDOW * SUB
    band_cols = own_rows // lat_rows

    @pl.when(step == 0)
    def _():
        w_pair = jnp.concatenate([wk[...], wv[...]], axis=1)

        def project(block):
            return dot(block[...], w_pair).astype(BF16).astype(F32)

        for ref, first, count in ((low, 0, edge), (lat, edge, own_rows), (high, edge + own_rows, edge)):
            block = project(ref)
            keys[pl.ds(first, count), :] = block[:, :attn]
            values[pl.ds(first, count), :] = block[:, attn:]
        keys[pl.ds(wide, SUB), :] = jnp.zeros((SUB, attn), F32)
        values[pl.ds(wide, SUB), :] = jnp.zeros((SUB, attn), F32)
        kg[...] = jnp.zeros_like(kg)
        vg[...] = jnp.zeros_like(vg)
        qg[...] = jnp.zeros_like(qg)
        outg[...] = jnp.zeros_like(outg)

    flat_x = x_ref[...].reshape(tiles * length, width)
    flat_cot = cot_ref[...].reshape(tiles * length, width)
    queries = dot(flat_x, wq[...]).astype(BF16)

    row_id = lax.broadcasted_iota(jnp.int32, (length, width), 0)
    lives = []
    for j in range(tiles):
        t = step * tiles + j
        used = jnp.sum(mask_ref[pl.ds(t, 1), :], axis=1, keepdims=True)
        used = jnp.where(t < cnt[0], used, 0)
        lives.append(row_id < used)
    live = jnp.concatenate([m.astype(F32) for m in lives], axis=0)
    masked = (flat_cot.astype(F32) * live).astype(BF16)
    att_grad = dot(masked, wo[...], NT).astype(BF16)

    lane = lax.broadcasted_iota(jnp.int32, (1, attn), 1) // head
    head_mask = [(lane == h).astype(F32) for h in range(HEADS)]
    slot_id = lax.broadcasted_iota(jnp.int32, (slots, length), 0)
    valid = ((slot_id & (SUB - 1)) < WINDOW)[None]
    band_first = lax.axis_index("lon") * band_cols

    att_parts, query_parts = [], []
    for j in range(tiles):
        t = step * tiles + j
        col = lax.rem(tw[0, t] - band_first + REACH + lon_cols, lon_cols)
        base = col * lat_rows + tw[1, t]
        q_t = queries[j * length : (j + 1) * length]
        g_t = att_grad[j * length : (j + 1) * length]
        spans = [pl.ds(base + a * lat_rows, SUB) for a in range(WINDOW)]
        kw = jnp.concatenate([keys[at, :] for at in spans], axis=0)
        vw = jnp.concatenate([values[at, :] for at in spans], axis=0)
        kb = jnp.concatenate([kw * m for m in head_mask], axis=0).astype(BF16)
        vb = jnp.concatenate([vw * m for m in head_mask], axis=0).astype(BF16)
        th = jnp.tanh(dot(kb, q_t, NT) * scale / CAP).reshape(HEADS, slots, length)
        e = jnp.where(valid, jnp.exp(CAP * th), 0.0)
        p = e * (1.0 / jnp.sum(e, axis=1, keepdims=True))
        dp = dot(vb, g_t, NT).reshape(HEADS, slots, length)
        inner = jnp.sum(p * dp, axis=1, keepdims=True)
        sg = p * (dp - inner) * (1.0 - th * th) * scale
        sg = sg.reshape(HEADS * slots, length).astype(BF16)
        pb = p.reshape(HEADS * slots, length).astype(BF16)
        att_parts.append(dot(pb, vb, TN).astype(BF16))
        query_parts.append(dot(sg, kb, TN).astype(BF16))
        kp = dot(sg, q_t)
        vp = dot(pb, g_t)
        k_sum = sum(kp[h * slots : (h + 1) * slots] * head_mask[h] for h in range(HEADS))
        v_sum = sum(vp[h * slots : (h + 1) * slots] * head_mask[h] for h in range(HEADS))
        for a, at in enumerate(spans):
            kg[at, :] = kg[at, :] + k_sum[a * SUB : (a + 1) * SUB]
            vg[at, :] = vg[at, :] + v_sum[a * SUB : (a + 1) * SUB]

    attended = jnp.concatenate(att_parts, axis=0)
    query_part = jnp.concatenate(query_parts, axis=0)
    dec[...] = (flat_x.astype(F32) + live * dot(attended, wo[...])).astype(BF16).reshape(dec.shape)
    og[...] = (flat_cot.astype(F32) + dot(query_part, wq[...], NT)).astype(BF16).reshape(og.shape)
    qg[...] += dot(flat_x, query_part, TN)
    outg[...] += dot(attended, masked, TN)

    @pl.when(step == pl.num_programs(0) - 1)
    def _():
        half = own_out.shape[1]
        parts = own_out.shape[0] // 2
        for ref, lanes in ((kg, pl.ds(0, attn)), (vg, pl.ds(attn, attn))):
            for k in range(2 * parts):
                own_out[k, :, lanes] = ref[pl.ds(edge + k * half, half), :].astype(BF16)
                at = k * half if k < parts else own_rows + k * half
                halo_out[k, :, lanes] = ref[pl.ds(at, half), :].astype(BF16)
        kv = jnp.zeros((width, 2 * attn), F32)
        for ref, first, count in ((low, 0, edge), (lat, edge, own_rows), (high, edge + own_rows, edge)):
            rows_at = pl.ds(first, count)
            grad = jnp.concatenate([kg[rows_at, :], vg[rows_at, :]], axis=1)
            grad_high = grad.astype(BF16)
            grad_low = (grad - grad_high.astype(F32)).astype(BF16)
            kv = kv + dot(ref[...], grad_high, TN) + dot(ref[...], grad_low, TN)
        rows = g_out.shape[1]
        pieces = (qg[...], kv[:, :attn], kv[:, attn:], outg[:, :attn], outg[:, attn:])
        at = 0
        for piece in pieces:
            count = piece.shape[0] // rows
            g_out[pl.ds(at, count)] = piece.astype(BF16).reshape(count, rows, attn)
            at += count


def reduce_kernel(
    n_inst, n_lon, parts, gp, own_hbm, halo_hbm, g_hbm, shares, ag, own, halo, g, load,
    pre, hsum, hbuf, share, rs, part, mine, gpre, gsum, b_s, b_r, h_s, h_r, i_s, i_r, rs_s, rs_r,
    p_s, p_r, a_s, a_r, f_s, f_r, local,
):
    me, mi = lax.axis_index("lon"), lax.axis_index("inst")
    slot = mi if parts > 1 else 0

    def lon_at(d):
        return lax.rem(me + d, n_lon)

    def inst_at(d):
        return lax.rem(mi + d, n_inst)

    loads = [
        pltpu.make_async_copy(src, dst, load.at[k])
        for k, (src, dst) in enumerate(((g_hbm, g), (halo_hbm, halo), (own_hbm, own)))
    ]
    for copy in loads:
        copy.start()
    barrier = pltpu.get_barrier_semaphore()
    for d in range(1, n_lon):
        pl.semaphore_signal(barrier, inc=1, device_id={"lon": lon_at(d)}, device_id_type=MESH)
    for d in range(1, n_inst):
        pl.semaphore_signal(barrier, inc=1, device_id={"inst": inst_at(d)}, device_id_type=MESH)
    pl.semaphore_wait(barrier, n_lon + n_inst - 2)

    for copy in loads:
        copy.wait()
    joined, presums = [], []
    if gp > 1:
        presums = [
            send(g.at[pl.ds(inst_at(d) * n_lon, n_lon)], gpre.at[d], p_s.at[d], p_r.at[d],
                 {"inst": inst_at(d)})
            for d in range(1, n_inst)
        ]
    if parts > 1:
        for side in range(2):
            for d in range(1, n_inst):
                joined.append(send(
                    halo.at[side * parts + inst_at(d)], pre.at[side, d], b_s.at[side, d],
                    b_r.at[side, d], {"inst": inst_at(d)}))
    if gp > 1:
        for copy in presums:
            copy.wait()
        total = g[pl.ds(mi * n_lon, n_lon)].astype(F32)
        for d in range(1, n_inst):
            total = total + gpre[d].astype(F32)
        gsum[...] = total.astype(BF16)
        source = gsum
    else:
        source = g
    scatters = [
        send(source.at[lon_at(d)], rs.at[d], rs_s.at[d], rs_r.at[d], {"lon": lon_at(d)})
        for d in range(1, n_lon)
    ]
    for copy in joined:
        copy.wait()
    halos = []
    for side, d in ((0, n_lon - 1), (1, 1)):
        total = halo[side * parts + slot].astype(F32)
        if parts > 1:
            for e in range(1, n_inst):
                total = total + pre[side, e].astype(F32)
        hsum[side] = total.astype(BF16)
        halos.append(send(
            hsum.at[side], hbuf.at[side], h_s.at[side], h_r.at[side], {"lon": lon_at(d)}))
    for k in range(2 * parts):
        share[k] = own[k]
    for copy in scatters:
        copy.wait()
    total = source[me].astype(F32)
    for d in range(1, n_lon):
        total = total + rs[d].astype(F32)
    if gp == 1:
        part[mi] = total
        swaps = [
            send(part.at[mi], part.at[mi], p_s.at[d], p_r.at[d], {"inst": inst_at(d)})
            for d in range(1, n_inst)
        ]
        for copy in swaps:
            copy.wait()
        total = part[0]
        for i in range(1, n_inst):
            total = total + part[i]
    mine[...] = total.astype(BF16)
    base = mi * n_lon if gp > 1 else 0
    gathers = [
        send(mine, ag.at[base + me], a_s.at[d], a_r.at[d], {"lon": lon_at(d)})
        for d in range(1, n_lon)
    ]
    fans = []
    if gp > 1:
        fans = [
            send(mine, ag.at[base + me], f_s.at[d, 0], f_r.at[d, 0], {"inst": inst_at(d)})
            for d in range(1, n_inst)
        ]
    keep = pltpu.make_async_copy(mine, ag.at[base + me], local.at[0])
    keep.start()
    for copy in halos:
        copy.wait()
    share[slot] = (own[slot].astype(F32) + hbuf[1].astype(F32)).astype(BF16)
    share[parts + slot] = (own[parts + slot].astype(F32) + hbuf[0].astype(F32)).astype(BF16)
    joins = [
        send(share, shares.at[mi], i_s.at[d], i_r.at[d], {"inst": inst_at(d)})
        for d in range(1, n_inst)
    ]
    joins.append(pltpu.make_async_copy(share, shares.at[mi], local.at[1]))
    joins[-1].start()
    for e, copy in enumerate(gathers, 1):
        copy.wait_recv()
        if gp > 1:
            at = base + lon_at(n_lon - e)
            for d in range(1, n_inst):
                fans.append(send(
                    ag.at[at], ag.at[at], f_s.at[d, e], f_r.at[d, e], {"inst": inst_at(d)}))
    for copy in gathers:
        copy.wait_send()
    for copy in joins + fans + [keep]:
        copy.wait()


def finish_kernel(lat_rows, shares, ag, wk, wv, lat_out, q_out, k_out, v_out, o_out):
    attn = wk.shape[1]
    grad = shares[0, 0].astype(F32)
    for i in range(1, shares.shape[0]):
        grad = grad + shares[i, 0].astype(F32)
    grad_high = grad.astype(BF16)
    grad_low = (grad - grad_high.astype(F32)).astype(BF16)
    w_pair = jnp.concatenate([wk[...], wv[...]], axis=1)
    lat_out[...] = dot(grad_high, w_pair, NT) + dot(grad_low, w_pair, NT)

    rows = ag.shape[1]
    step, steps = pl.program_id(0), lat_rows // lat_out.shape[0]
    at = 0
    out_parts = [o_out.at[:, pl.ds(0, attn)], o_out.at[:, pl.ds(attn, attn)]]
    for out in [q_out, k_out, v_out] + out_parts:
        count = out.shape[0] // rows
        out[...] = ag[pl.ds(at + step * count, count)].astype(F32).reshape(out.shape)
        at += steps * count


def vmem():
    return pl.BlockSpec(memory_space=pltpu.VMEM)


def shards(
    n_inst, n_lon, obs_x, obs_cot, tile_window, point_mask, band_counts, latents,
    w_query, w_key, w_value, w_out,
):
    n_tiles, length, width = obs_x.shape
    band_cols, lat_rows, _ = latents.shape
    attn = w_query.shape[1]
    edge, own_rows = REACH * lat_rows, band_cols * lat_rows
    wide = own_rows + 2 * edge
    flat = latents.reshape(own_rows, width)
    parts = n_inst if edge % (SUB * n_inst) == 0 else 1
    half = edge // parts
    dma = pltpu.SemaphoreType.DMA
    anywhere = pl.BlockSpec(memory_space=pl.ANY)
    group = next(b for b in (4, 3, 2, 1) if n_tiles % b == 0)
    smem = pl.BlockSpec(memory_space=pltpu.SMEM)
    low, high = pl.pallas_call(
        functools.partial(halo_kernel, n_inst, n_lon, parts),
        out_shape=[jax.ShapeDtypeStruct((parts, half, width), BF16)] * 2,
        in_specs=[anywhere],
        out_specs=[anywhere] * 2,
        scratch_shapes=[dma((2,)), dma((2,)), dma((2, n_inst)), dma((2, n_inst))],
        compiler_params=pltpu.CompilerParams(collective_id=0, has_side_effects=True),
        name="halo",
    )(latents.reshape(2 * parts, half, width))
    low, high = low.reshape(edge, width), high.reshape(edge, width)

    weight_rows = 2 * width + 2 * attn + width
    rows = weight_rows // n_lon
    gp = n_inst if rows % (2 * SUB * n_inst) == 0 else 1
    rows = rows // gp
    whole = lambda *shape: pl.BlockSpec(shape, lambda i: (0,) * len(shape))
    tile_spec = pl.BlockSpec((group, length, width), lambda i: (i, 0, 0))
    decoded, obs_grad, own, halo, g = pl.pallas_call(
        functools.partial(attend_kernel, band_cols * n_lon, lat_rows),
        grid=(n_tiles // group,),
        out_shape=[
            jax.ShapeDtypeStruct(obs_x.shape, BF16),
            jax.ShapeDtypeStruct(obs_x.shape, BF16),
            jax.ShapeDtypeStruct((2 * parts, half, 2 * attn), BF16),
            jax.ShapeDtypeStruct((2 * parts, half, 2 * attn), BF16),
            jax.ShapeDtypeStruct((gp * n_lon, rows, attn), BF16),
        ],
        in_specs=[
            smem, smem, tile_spec, tile_spec, whole(n_tiles, length), whole(own_rows, width),
            whole(edge, width), whole(edge, width), whole(width, attn), whole(width, attn),
            whole(width, attn), whole(attn, width),
        ],
        out_specs=[
            tile_spec, tile_spec, whole(2 * parts, half, 2 * attn), whole(2 * parts, half, 2 * attn),
            whole(gp * n_lon, rows, attn),
        ],
        scratch_shapes=[
            pltpu.VMEM((wide + SUB, attn), F32),
            pltpu.VMEM((wide + SUB, attn), F32),
            pltpu.VMEM((wide + SUB, attn), F32),
            pltpu.VMEM((wide + SUB, attn), F32),
            pltpu.VMEM((width, attn), F32),
            pltpu.VMEM((attn, width), F32),
        ],
        name="attend",
    )(tile_window.T, band_counts, obs_x, obs_cot, point_mask, flat, low, high,
      w_query, w_key, w_value, w_out)

    shares, ag = pl.pallas_call(
        functools.partial(reduce_kernel, n_inst, n_lon, parts, gp),
        out_shape=[
            jax.ShapeDtypeStruct((n_inst, 2 * parts, half, 2 * attn), BF16),
            jax.ShapeDtypeStruct((gp * n_lon, rows, attn), BF16),
        ],
        in_specs=[anywhere] * 3,
        out_specs=[anywhere] * 2,
        scratch_shapes=[
            pltpu.VMEM((2 * parts, half, 2 * attn), BF16),
            pltpu.VMEM((2 * parts, half, 2 * attn), BF16),
            pltpu.VMEM((gp * n_lon, rows, attn), BF16),
            dma((3,)),
            pltpu.VMEM((2, n_inst, half, 2 * attn), BF16),
            pltpu.VMEM((2, half, 2 * attn), BF16),
            pltpu.VMEM((2, half, 2 * attn), BF16),
            pltpu.VMEM((2 * parts, half, 2 * attn), BF16),
            pltpu.VMEM((n_lon, rows, attn), BF16),
            pltpu.VMEM((n_inst, rows, attn), F32),
            pltpu.VMEM((rows, attn), BF16),
            pltpu.VMEM((n_inst, n_lon, rows, attn), BF16),
            pltpu.VMEM((n_lon, rows, attn), BF16),
            dma((2, n_inst)), dma((2, n_inst)),
            dma((2,)), dma((2,)),
            dma((n_inst,)), dma((n_inst,)),
            dma((n_lon,)), dma((n_lon,)),
            dma((n_inst,)), dma((n_inst,)),
            dma((n_lon,)), dma((n_lon,)),
            dma((n_inst, n_lon)), dma((n_inst, n_lon)),
            dma((2,)),
        ],
        compiler_params=pltpu.CompilerParams(collective_id=1, has_side_effects=True),
        name="reduce",
    )(own, halo, g)
    latent_grad, query_grad, key_grad, value_grad, out_grad = pl.pallas_call(
        functools.partial(finish_kernel, own_rows),
        grid=(2 * parts,),
        out_shape=[
            jax.ShapeDtypeStruct((own_rows, width), F32),
            jax.ShapeDtypeStruct((width, attn), F32),
            jax.ShapeDtypeStruct((width, attn), F32),
            jax.ShapeDtypeStruct((width, attn), F32),
            jax.ShapeDtypeStruct((attn, width), F32),
        ],
        in_specs=[
            pl.BlockSpec((n_inst, 1, half, 2 * attn), lambda i: (0, i, 0, 0)),
            whole(gp * n_lon, rows, attn), whole(width, attn), whole(width, attn),
        ],
        out_specs=[
            pl.BlockSpec((half, width), lambda i: (i, 0)),
            *[pl.BlockSpec((width // (2 * parts), attn), lambda i: (i, 0))] * 3,
            pl.BlockSpec((attn // (2 * parts), width), lambda i: (i, 0)),
        ],
        name="finish",
    )(shares, ag, w_key, w_value)
    return (
        decoded,
        obs_grad,
        latent_grad.reshape(band_cols, lat_rows, width),
        query_grad,
        key_grad,
        value_grad,
        out_grad,
    )


def solution(mesh):
    placed = (
        P(("inst", "lon"), None, None),
        P(("inst", "lon"), None, None),
        P(("inst", "lon"), None),
        P(("inst", "lon"), None),
        P(("inst", "lon")),
        P("lon", None, None),
        P(),
        P(),
        P(),
        P(),
    )
    return jax.shard_map(
        functools.partial(shards, mesh.shape["inst"], mesh.shape["lon"]),
        mesh=mesh,
        in_specs=placed,
        out_specs=(
            P(("inst", "lon"), None, None),
            P(("inst", "lon"), None, None),
            P("lon", None, None),
            P(),
            P(),
            P(),
            P(),
        ),
        check_vma=False,
    )
```
